32 devices in a mesh: groups: 2 (over y), seq: 4 (over z), head: 4 (over x, core).
Axes of the slice: x: 2, y: 2, z: 4, core: 2. Of those that a mesh axis runs over, the one named last changes fastest.
Arguments:
- query: bfloat16 [16, 1024, 128], P('head', ('groups', 'seq')), parts along dimension 1, may hold values from -400 to 400
- keys: bfloat16 [4, 1024, 128], P('head', ('groups', 'seq')), parts along dimension 1, may hold values from -5 to 5
- values: bfloat16 [4, 1024, 128], P('head', ('groups', 'seq')), parts along dimension 1, may hold values from -6 to 6
- ratio: bfloat16 [16, 1024, 128], P('head', ('groups', 'seq')), parts along dimension 1, may hold values from -4 to 4
- block_order: int32 [16], P('groups'), parts along dimension 0, may hold values from 0 to 7, each once
Outputs:
- query_rel: float32 [16, 1024, 128], P('head', ('groups', 'seq')), parts along dimension 1
- key_rel: float32 [4, 1024, 128], P('head', ('groups', 'seq')), parts along dimension 1
- value_rel: float32 [4, 1024, 128], P('head', ('groups', 'seq')), parts along dimension 1
The draws below stay inside these ranges and needn't reach their ends.
There are 2 independent parts, one for each index of `groups`. The reference program is written for one: setup_inputs(seed, part) draws one part's arguments, and reference() takes and returns one part's arrays. A program takes and returns all parts, laid end to end along the dimension named above; each array names one. Nothing has to cross between parts.
Inputs may be any that keep to these rules, and one draw needn't show every extreme that they name: A permutation: stored block b holds prompt block block_order[b], each once.
All inputs are finite; a program needn't handle non-finite values.
Results may differ from the reference program's by a relative error of at most 0.04.
Values may be sent and summed in bfloat16 or wider, within the bound.
No kernel may reach another device: no remote copies, remote signals or barrier semaphores. Data moves between devices by JAX's collectives and lax.ppermute only.
A program may use at most 64 MiB of HBM per device.

```python
import jax
import jax.numpy as jnp
from jax import lax

HD = 128
QPK = 4
KVH = 4
QH = 16
TOKENS = 512
BLK = 64
NBLK = 8


def query_and_keys(key):
    base = jax.random.fold_in(key, 11)
    first_key, second_key = jax.random.split(base, 2)
    keys = jnp.clip(jax.random.normal(first_key, (KVH, TOKENS, HD), jnp.float32), -4.0, 4.0)
    query = jnp.clip(jax.random.normal(second_key, (QH, TOKENS, HD), jnp.float32), -4.0, 4.0)
    return (query, keys)


def draw_query(key, part):
    return query_and_keys(key)[0].astype(jnp.bfloat16)


def draw_keys(key, part):
    return query_and_keys(key)[1].astype(jnp.bfloat16)


def shard_levels(own_key, dims, pieces, least, top_value):
    level = 1.0
    for dim, parts in pieces:
        draws = jax.random.uniform(jax.random.fold_in(jax.random.fold_in(own_key, 6), dim), (parts,), jnp.float32, least / len(pieces), top_value / len(pieces))
        level = level * jnp.repeat(jnp.exp(draws), dims[dim] // parts).reshape((-1,) + (1,) * (len(dims) - 1 - dim))
    return level


def normal_values(own_key, shape, scale, limit, shards=(), kind=jnp.bfloat16):
    level = shard_levels(own_key, shape, shards, -0.22, 0.18) if shards else 1.0
    array = jax.random.normal(own_key, shape, jnp.float32) * scale * level
    return jnp.minimum(jnp.maximum(array, -limit), limit).astype(kind)


def setup_inputs(seed: int = 0, part: int = 0) -> dict:
    seeds = jax.random.split(jax.random.key(seed), 6)
    part_splits = jax.random.split(jax.random.fold_in(seeds[5], part), 6)
    return {
        "query": draw_query(jax.random.fold_in(jax.random.fold_in(seeds[5], part), 71), part),
        "keys": draw_keys(jax.random.fold_in(jax.random.fold_in(seeds[5], part), 71), part),
        "values": normal_values(part_splits[2], (KVH, TOKENS, HD), 1.0, 6.0, ((0, 4), (1, 4))),
        "ratio": normal_values(part_splits[3], (QH, TOKENS, HD), 0.5, 4.0, ((0, 4), (1, 4))),
        "block_order": jax.random.permutation(part_splits[4], NBLK).astype(jnp.int32),
    }


def token_places(block_order):
    offsets = jnp.arange(BLK, dtype=jnp.int32)
    return (block_order[:, None] * BLK + offsets[None, :]).reshape(-1)


def reference(query, keys, values, ratio, block_order):
    score_scale = HD ** -0.5
    places = token_places(block_order)
    visible = places[None, :] <= places[:, None]
    grouped_query = query.reshape(KVH, QPK, TOKENS, HD)
    grouped_ratio = ratio.reshape(KVH, QPK, TOKENS, HD)

    def one_group(operands):
        query_heads, ratio_heads, key_rows, value_rows = operands

        def one_head(head_pair):
            query_rows, ratio_rows = head_pair
            scores = jnp.dot(query_rows, key_rows.T, preferred_element_type=jnp.float32) * score_scale
            scores = jnp.where(visible, scores, -jnp.inf)
            row_top = jnp.max(scores, axis=1, keepdims=True)
            exp_scores = jnp.exp(scores - row_top)
            weights = exp_scores / jnp.sum(exp_scores, axis=1, keepdims=True)
            prob_grad = jnp.dot(ratio_rows, value_rows.T, preferred_element_type=jnp.float32)
            row_expect = jnp.sum(weights * prob_grad, axis=1, keepdims=True)
            soft_grad = (weights * (prob_grad - row_expect)).astype(jnp.bfloat16)
            low_weights = weights.astype(jnp.bfloat16)
            query_part = 0.5 * score_scale * query_rows.astype(jnp.float32) * jnp.dot(soft_grad, key_rows, preferred_element_type=jnp.float32)
            key_part = jnp.dot(soft_grad.T, query_rows, preferred_element_type=jnp.float32)
            value_part = jnp.dot(low_weights.T, ratio_rows, preferred_element_type=jnp.float32)
            return query_part, key_part, value_part

        query_part, key_part, value_part = lax.map(one_head, (query_heads, ratio_heads))
        key_out = 0.5 * score_scale * key_rows.astype(jnp.float32) * jnp.sum(key_part, axis=0)
        value_out = value_rows.astype(jnp.float32) * jnp.sum(value_part, axis=0)
        return query_part, key_out, value_out

    query_rel, key_rel, value_rel = lax.map(one_group, (grouped_query, grouped_ratio, keys, values))
    return query_rel.reshape(QH, TOKENS, HD), key_rel, value_rel
```

```python
import functools
import math

import jax
import jax.numpy as jnp
from jax import lax
from jax.experimental import pallas as pl
from jax.experimental.pallas import tpu as pltpu
from jax.sharding import PartitionSpec as P

F32 = jnp.float32
BF16 = jnp.bfloat16
HIDDEN = -1e30
FEW = 8
LOG2E = math.log2(math.e)


def dot(a, b, dims):
    return lax.dot_general(a, b, (dims, ((), ())), preferred_element_type=F32)


def each(count, step, unrolled):
    if unrolled:
        for slot in range(count):
            step(slot)
    else:
        lax.fori_loop(0, count, lambda slot, _: (step(slot), None)[1], None)


def main_kernel(
    shape, scale, order_ref, owner_ref, query_ref, ratio_ref, key_ref, value_ref, *rest
):
    slots, blocks, block_rows, joined = shape
    rows = blocks * block_rows
    queries = query_ref.shape[0]
    if joined:
        (seen_ref, terms_ref, soft_ref, score_ref, grad_ref) = rest
    else:
        seen = rest[: slots - 1]
        terms = rest[slots - 1 : 2 * slots - 1]
        soft_ref, score_ref, grad_ref = rest[2 * slots - 1 :]
    head = query_ref.shape[1]

    def keys_of(slot):
        if joined:
            return seen_ref[slot, :, :head]
        return key_ref[...] if slot == 0 else seen[slot - 1][:, :head]

    def values_of(slot):
        if joined:
            return seen_ref[slot, :, head:]
        return value_ref[...] if slot == 0 else seen[slot - 1][:, head:]

    def rows_of(slot):
        return pl.ds(pl.multiple_of(slot * rows, rows), rows)

    lane = lax.broadcasted_iota(jnp.int32, (1, queries), 1) % rows
    mine = owner_ref[slots]
    places = lane % block_rows
    for block in range(blocks):
        first = order_ref[mine * blocks + block] * block_rows
        places = places + jnp.where(lane // block_rows == block, first, 0)
    inner = lax.broadcasted_iota(jnp.int32, (block_rows, queries), 0)

    def scores(slot):
        found = dot(keys_of(slot), query_ref[...], ((1,), (1,)))
        parts = []
        for block in range(blocks):
            first = order_ref[owner_ref[slot] * blocks + block] * block_rows
            part = found[block * block_rows : (block + 1) * block_rows]
            parts.append(jnp.where(inner <= places - first, part, HIDDEN))
        found = jnp.concatenate(parts, axis=0)
        score_ref[rows_of(slot), :] = found
        grad_ref[rows_of(slot), :] = dot(values_of(slot), ratio_ref[...], ((1,), (1,)))
        return jnp.max(found.reshape(rows // 8, 8, queries), axis=0)

    def exps(slot, top):
        power = jnp.exp2((score_ref[rows_of(slot), :] - top) * (scale * LOG2E))
        score_ref[rows_of(slot), :] = power
        weighted = power * grad_ref[rows_of(slot), :]
        return (
            jnp.sum(power.reshape(rows // 8, 8, queries), axis=0),
            jnp.sum(weighted.reshape(rows // 8, 8, queries), axis=0),
        )

    if joined:
        top = lax.fori_loop(
            0,
            slots,
            lambda slot, top: jnp.maximum(top, scores(slot)),
            jnp.full((8, queries), HIDDEN, F32),
        )
    else:
        top = functools.reduce(jnp.maximum, [scores(slot) for slot in range(slots)])
    top = jnp.max(top, axis=0, keepdims=True)
    if joined:
        zero = jnp.zeros((8, queries), F32)

        def add(slot, sums):
            total, weighted = exps(slot, top)
            return sums[0] + total, sums[1] + weighted

        total, weighted = lax.fori_loop(0, slots, add, (zero, zero))
    else:
        sums = [exps(slot, top) for slot in range(slots)]
        total = functools.reduce(jnp.add, [one for one, _ in sums])
        weighted = functools.reduce(jnp.add, [one for _, one in sums])
    share = 1.0 / jnp.sum(total, axis=0, keepdims=True)
    expect = jnp.sum(weighted, axis=0, keepdims=True) * share

    def finish(slot):
        weights = score_ref[rows_of(slot), :] * share
        soft = (weights * (grad_ref[rows_of(slot), :] - expect)).astype(BF16)
        soft_ref[rows_of(slot), :] = soft
        key_part = dot(soft, query_ref[...], ((1,), (0,)))
        value_part = dot(weights.astype(BF16), ratio_ref[...], ((1,), (0,)))
        if joined:
            terms_ref[slot, :, :head] = key_part
            terms_ref[slot, :, head:] = value_part
        else:
            terms[slot][:, :head] = key_part.astype(terms[slot].dtype)
            terms[slot][:, head:] = value_part.astype(terms[slot].dtype)

    if joined:
        each(slots, finish, False)
    else:
        for slot in (*range(1, slots), 0):
            finish(slot)


def query_kernel(shape, factor, query_ref, soft_ref, key_ref, *rest):
    slots, rows, joined = shape
    *seen, out_ref = rest
    head = query_ref.shape[1]

    def part(slot, keys):
        soft = soft_ref[pl.ds(pl.multiple_of(slot * rows, rows), rows), :]
        return dot(soft, keys, ((0,), (0,)))

    if joined:
        out_ref[...] = jnp.zeros_like(out_ref)

        def add(slot):
            out_ref[...] += part(slot, seen[0][slot, :, :head])

        each(slots, add, False)
        found = out_ref[...]
    else:
        found = part(0, key_ref[...])
        for slot in range(1, slots):
            found += part(slot, seen[slot - 1][:, :head])
    out_ref[...] = factor * query_ref[...].astype(F32) * found


def sum_kernel(factor, key_ref, value_ref, own_ref, *rest):
    *got, key_out, value_out = rest
    head = key_ref.shape[1]
    total = own_ref[...]
    for one in got:
        total = total + one[...].astype(F32)
    key_out[...] = factor * key_ref[...].astype(F32) * total[:, :head]
    value_out[...] = value_ref[...].astype(F32) * total[:, head:]


def body(query, keys, values, ratio, block_order):
    kv_heads, rows, head = keys.shape
    group = query.shape[0] // kv_heads
    queries = group * rows
    scale = head ** (-0.5)
    slots = lax.axis_size("seq")
    mine = lax.axis_index("seq")
    blocks = block_order.shape[0] // slots
    block_rows = rows // blocks
    joined = slots > FEW
    swap = slots & (slots - 1) == 0
    limit = min(60 << 20, (8 << 20) + 16 * slots * rows * queries)
    smem = pl.BlockSpec(memory_space=pltpu.SMEM)
    vmem = pl.BlockSpec(memory_space=pltpu.VMEM)

    def partner(step):
        return mine ^ step if swap else lax.rem(mine - step + slots, slots)

    def pairs(step, back):
        if swap:
            return [(device, device ^ step) for device in range(slots)]
        step = -step if back else step
        return [(device, (device + step) % slots) for device in range(slots)]

    def one_head(query_rows, ratio_rows, key_rows, value_rows):
        both = jnp.concatenate((key_rows, value_rows), axis=1)
        if joined:
            owners = jnp.append(jnp.arange(slots, dtype=jnp.int32), mine)
            seen = [lax.all_gather(both, "seq")]
            terms_shape = [jax.ShapeDtypeStruct((slots, rows, 2 * head), F32)]
        else:
            owners = jnp.stack([partner(step) if step else mine for step in range(slots)] + [mine])
            seen = [lax.ppermute(both, "seq", pairs(step, False)) for step in range(1, slots)]
            terms_shape = [
                jax.ShapeDtypeStruct((rows, 2 * head), BF16 if step else F32) for step in range(slots)
            ]
        *terms, soft = pl.pallas_call(
            functools.partial(main_kernel, (slots, blocks, block_rows, joined), scale),
            out_shape=(*terms_shape, jax.ShapeDtypeStruct((slots * rows, queries), BF16)),
            in_specs=[smem, smem] + [vmem] * (4 + len(seen)),
            out_specs=tuple([vmem] * (len(terms_shape) + 1)),
            scratch_shapes=[
                pltpu.VMEM((slots * rows, queries), F32),
                pltpu.VMEM((slots * rows, queries), F32),
            ],
            compiler_params=pltpu.CompilerParams(vmem_limit_bytes=limit),
            cost_estimate=pl.CostEstimate(
                flops=8 * slots * rows * queries * head,
                bytes_accessed=4 * slots * rows * queries,
                transcendentals=slots * rows * queries,
            ),
        )(block_order, owners.astype(jnp.int32), query_rows, ratio_rows, key_rows, value_rows, *seen)
        if joined:
            own = lax.psum_scatter(terms[0], "seq", scatter_dimension=0, tiled=False)
            got = []
        else:
            own = terms[0]
            got = [lax.ppermute(terms[step], "seq", pairs(step, True)) for step in range(1, slots)]
        query_out = pl.pallas_call(
            functools.partial(query_kernel, (slots, rows, joined), 0.5 * scale),
            out_shape=jax.ShapeDtypeStruct((queries, head), F32),
            in_specs=[vmem] * (3 + len(seen)),
            out_specs=vmem,
            compiler_params=pltpu.CompilerParams(vmem_limit_bytes=limit),
            cost_estimate=pl.CostEstimate(
                flops=2 * slots * rows * queries * head,
                bytes_accessed=2 * slots * rows * queries,
                transcendentals=0,
            ),
        )(query_rows, soft, key_rows, *seen)
        key_out, value_out = pl.pallas_call(
            functools.partial(sum_kernel, 0.5 * scale),
            out_shape=(jax.ShapeDtypeStruct((rows, head), F32),) * 2,
            in_specs=[vmem] * (3 + len(got)),
            out_specs=(vmem, vmem),
            compiler_params=pltpu.CompilerParams(vmem_limit_bytes=limit),
        )(key_rows, value_rows, own, *got)
        return query_out.reshape(group, rows, head), key_out, value_out

    results = [
        one_head(
            query[g * group : (g + 1) * group].reshape(queries, head),
            ratio[g * group : (g + 1) * group].reshape(queries, head),
            keys[g],
            values[g],
        )
        for g in range(kv_heads)
    ]
    return (
        jnp.concatenate([one for one, _, _ in results], axis=0),
        jnp.stack([one for _, one, _ in results], axis=0),
        jnp.stack([one for _, _, one in results], axis=0),
    )


def solution(mesh):
    spec = P("head", ("groups", "seq"), None)
    return jax.shard_map(
        body,
        mesh=mesh,
        in_specs=(spec, spec, spec, spec, P("groups")),
        out_specs=(spec, spec, spec),
        check_vma=False,
    )
```

```python
import functools
import math

import jax
import jax.numpy as jnp
from jax import lax
from jax.experimental import pallas as pl
from jax.experimental.pallas import tpu as pltpu
from jax.sharding import PartitionSpec as P


F32 = jnp.float32
BF16 = jnp.bfloat16
HIDDEN = -1e30
FEW = 8
LOG2E = math.log2(math.e)
KEYS_FIRST = (2, 3, 1)
TERMS_FIRST = (2, 3, 1)


def dot(a, b, dims):
    return lax.dot_general(a, b, (dims, ((), ())), preferred_element_type=F32)


def folded(combine, tile):
    return combine(tile.reshape(tile.shape[0] // 8, 8, tile.shape[1]), axis=0)


def masked_scores(blocks, block_rows, order_ref, mine, owner, query, keys):
    rows, queries = blocks * block_rows, query.shape[0]
    lane = lax.broadcasted_iota(jnp.int32, (1, queries), 1) % rows
    places = lane % block_rows
    for block in range(blocks):
        first = order_ref[mine * blocks + block] * block_rows
        places = places + jnp.where(lane // block_rows == block, first, 0)
    inner = lax.broadcasted_iota(jnp.int32, (block_rows, queries), 0)
    found = dot(keys, query, ((1,), (1,)))
    parts = []
    for block in range(blocks):
        first = order_ref[owner * blocks + block] * block_rows
        part = found[block * block_rows : (block + 1) * block_rows]
        parts.append(jnp.where(inner <= places - first, part, HIDDEN))
    return jnp.concatenate(parts, axis=0)


def block_softmax(blocks, block_rows, scale, slot, order_ref, owner_ref, query, ratio, both):
    head = query.shape[1]
    found = masked_scores(
        blocks, block_rows, order_ref, owner_ref[0], owner_ref[slot], query, both[:, :head]
    )
    top = jnp.max(folded(jnp.max, found), axis=0, keepdims=True)
    power = jnp.exp2((found - top) * (scale * LOG2E))
    grad = dot(both[:, head:], ratio, ((1,), (1,)))
    total = jnp.sum(folded(jnp.sum, power), axis=0, keepdims=True)
    weighted = jnp.sum(folded(jnp.sum, power * grad), axis=0, keepdims=True)
    return power, grad, (top, total, weighted)


def block_kernel(shape, scale, slot, order_ref, owner_ref, query_ref, ratio_ref, both_ref, power_ref, grad_ref, stat_ref):
    power, grad, stats = block_softmax(
        *shape, scale, slot, order_ref, owner_ref, query_ref[...], ratio_ref[...], both_ref[...]
    )
    power_ref[...] = power
    grad_ref[...] = grad
    for row, stat in enumerate(stats):
        stat_ref[row : row + 1, :] = stat


def finish(power, grad, share, expect, query, ratio):
    weights = power * share
    soft = (weights * (grad - expect)).astype(BF16)
    key_part = dot(soft, query, ((1,), (0,)))
    value_part = dot(weights.astype(BF16), ratio, ((1,), (0,)))
    return soft, key_part, value_part


def last_kernel(shape, scale, slot, others, order_ref, owner_ref, query_ref, ratio_ref, both_ref, *rest):
    *stat_refs, term_ref, soft_ref, norm_ref = rest
    head = query_ref.shape[1]
    query, ratio = query_ref[...], ratio_ref[...]
    power, grad, own_stats = block_softmax(
        *shape, scale, slot, order_ref, owner_ref, query, ratio, both_ref[...]
    )
    stats = {slot: own_stats}
    for other, ref in zip(others, stat_refs):
        stats[other] = (ref[0:1, :], ref[1:2, :], ref[2:3, :])
    top = functools.reduce(jnp.maximum, [stat[0] for stat in stats.values()])
    shares = {one: jnp.exp2((stat[0] - top) * (scale * LOG2E)) for one, stat in stats.items()}
    total = functools.reduce(jnp.add, [shares[one] * stats[one][1] for one in stats])
    weighted = functools.reduce(jnp.add, [shares[one] * stats[one][2] for one in stats])
    whole = 1.0 / total
    expect = weighted * whole
    for other in others:
        norm_ref[other : other + 1, :] = shares[other] * whole
    norm_ref[slot : slot + 1, :] = expect
    soft, key_part, value_part = finish(power, grad, shares[slot] * whole, expect, query, ratio)
    soft_ref[...] = soft
    term_ref[:, :head] = key_part.astype(BF16)
    term_ref[:, head:] = value_part.astype(BF16)


def term_kernel(slot, last, query_ref, ratio_ref, power_ref, grad_ref, norm_ref, term_ref, soft_ref):
    head = query_ref.shape[1]
    soft, key_part, value_part = finish(
        power_ref[...],
        grad_ref[...],
        norm_ref[slot : slot + 1, :],
        norm_ref[last : last + 1, :],
        query_ref[...],
        ratio_ref[...],
    )
    soft_ref[...] = soft
    term_ref[:, :head] = key_part.astype(term_ref.dtype)
    term_ref[:, head:] = value_part.astype(term_ref.dtype)


def own_kernel(factor, last, query_ref, ratio_ref, power_ref, grad_ref, norm_ref, both_ref, *rest):
    *pairs, own_ref, out_ref = rest
    head = query_ref.shape[1]
    soft, key_part, value_part = finish(
        power_ref[...],
        grad_ref[...],
        norm_ref[0:1, :],
        norm_ref[last : last + 1, :],
        query_ref[...],
        ratio_ref[...],
    )
    own_ref[:, :head] = key_part
    own_ref[:, head:] = value_part
    found = dot(soft, both_ref[:, :head], ((0,), (0,)))
    for soft_ref, seen_ref in zip(pairs[::2], pairs[1::2]):
        found += dot(soft_ref[...], seen_ref[:, :head], ((0,), (0,)))
    out_ref[...] = factor * query_ref[...].astype(F32) * found


def sum_kernel(factor, both_ref, own_ref, *rest):
    *got, key_out, value_out = rest
    head = key_out.shape[1]
    total = own_ref[...]
    for one in got:
        total = total + one[...].astype(F32)
    key_out[...] = factor * both_ref[:, :head].astype(F32) * total[:, :head]
    value_out[...] = both_ref[:, head:].astype(F32) * total[:, head:]


def whole_kernel(shape, scale, order_ref, owner_ref, query_ref, ratio_ref, seen_ref, terms_ref, out_ref, score_ref, grad_ref):
    slots, blocks, block_rows = shape
    rows = blocks * block_rows
    queries, head = query_ref.shape
    query, ratio = query_ref[...], ratio_ref[...]

    def rows_of(slot):
        return pl.ds(pl.multiple_of(slot * rows, rows), rows)

    def scores(slot, top):
        found = masked_scores(
            blocks, block_rows, order_ref, owner_ref[0], slot, query, seen_ref[slot, :, :head]
        )
        score_ref[rows_of(slot), :] = found
        grad_ref[rows_of(slot), :] = dot(seen_ref[slot, :, head:], ratio, ((1,), (1,)))
        return jnp.maximum(top, folded(jnp.max, found))

    top = lax.fori_loop(0, slots, scores, jnp.full((8, queries), HIDDEN, F32))
    top = jnp.max(top, axis=0, keepdims=True)
    zero = jnp.zeros((8, queries), F32)

    def exps(slot, sums):
        power = jnp.exp2((score_ref[rows_of(slot), :] - top) * (scale * LOG2E))
        score_ref[rows_of(slot), :] = power
        weighted = power * grad_ref[rows_of(slot), :]
        return sums[0] + folded(jnp.sum, power), sums[1] + folded(jnp.sum, weighted)

    total, weighted = lax.fori_loop(0, slots, exps, (zero, zero))
    share = 1.0 / jnp.sum(total, axis=0, keepdims=True)
    expect = jnp.sum(weighted, axis=0, keepdims=True) * share
    out_ref[...] = jnp.zeros_like(out_ref)

    def terms(slot, carry):
        soft, key_part, value_part = finish(
            score_ref[rows_of(slot), :], grad_ref[rows_of(slot), :], share, expect, query, ratio
        )
        terms_ref[slot, :, :head] = key_part
        terms_ref[slot, :, head:] = value_part
        out_ref[...] += dot(soft, seen_ref[slot, :, :head], ((0,), (0,)))
        return carry

    lax.fori_loop(0, slots, terms, 0)
    out_ref[...] = 0.5 * scale * query.astype(F32) * out_ref[...]


def body(query, keys, values, ratio, block_order):
    kv_heads, rows, head = keys.shape
    group = query.shape[0] // kv_heads
    queries = group * rows
    scale = head ** (-0.5)
    slots = lax.axis_size("seq")
    mine = lax.axis_index("seq")
    blocks = block_order.shape[0] // slots
    block_rows = rows // blocks
    shape = (blocks, block_rows)
    swap = slots & (slots - 1) == 0
    limit = min(60 << 20, (8 << 20) + 16 * slots * rows * queries)
    params = pltpu.CompilerParams(vmem_limit_bytes=limit)
    smem = pl.BlockSpec(memory_space=pltpu.SMEM)
    vmem = pl.BlockSpec(memory_space=pltpu.VMEM)
    tile = jax.ShapeDtypeStruct((rows, queries), F32)
    low_tile = jax.ShapeDtypeStruct((rows, queries), BF16)
    stat = jax.ShapeDtypeStruct((8, queries), F32)
    low_term = jax.ShapeDtypeStruct((rows, 2 * head), BF16)
    term = jax.ShapeDtypeStruct((rows, 2 * head), F32)
    part = jax.ShapeDtypeStruct((rows, head), F32)
    rel = jax.ShapeDtypeStruct((queries, head), F32)

    def run(kernel, outs, scalars, arrays, dots, scratch=()):
        single = not isinstance(outs, tuple)
        return pl.pallas_call(
            kernel,
            out_shape=outs,
            in_specs=[smem] * len(scalars) + [vmem] * len(arrays),
            out_specs=vmem if single else (vmem,) * len(outs),
            scratch_shapes=scratch,
            compiler_params=params,
            cost_estimate=pl.CostEstimate(
                flops=2 * dots * rows * queries * head,
                bytes_accessed=4 * dots * rows * queries,
                transcendentals=rows * queries,
            ),
        )(*scalars, *arrays)

    def pairs(step, back):
        if swap:
            return [(device, device ^ step) for device in range(slots)]
        step = -step if back else step
        return [(device, (device + step) % slots) for device in range(slots)]

    def many(query_rows, ratio_rows, both):
        seen = lax.all_gather(both, "seq")
        terms, query_out = run(
            functools.partial(whole_kernel, (slots, *shape), scale),
            (jax.ShapeDtypeStruct((slots, rows, 2 * head), F32), rel),
            (block_order, mine.reshape(1)),
            (query_rows, ratio_rows, seen),
            5 * slots,
            [pltpu.VMEM((slots * rows, queries), F32)] * 2,
        )
        own = lax.psum_scatter(terms, "seq", scatter_dimension=0, tiled=False)
        return own, [], query_out

    def few(query_rows, ratio_rows, both):
        steps = range(1, slots)
        first = KEYS_FIRST if slots == len(KEYS_FIRST) + 1 else tuple(steps)
        then = TERMS_FIRST if slots == len(TERMS_FIRST) + 1 else tuple(steps)
        last = then[0]
        others = [slot for slot in (0, *first) if slot != last]
        seen = {0: both}
        for step in first:
            seen[step] = lax.ppermute(both, "seq", pairs(step, False))
        device = jnp.arange(slots, dtype=jnp.int32)
        owners = mine ^ device if swap else lax.rem(mine - device + slots, slots)
        power, grad, stats = {}, {}, {}
        for slot in others:
            power[slot], grad[slot], stats[slot] = run(
                functools.partial(block_kernel, shape, scale, slot),
                (tile, tile, stat),
                (block_order, owners),
                (query_rows, ratio_rows, seen[slot]),
                2,
            )
        terms, soft, got = {}, {}, {}
        for slot in then:
            if slot == last:
                terms[slot], soft[slot], norm = run(
                    functools.partial(last_kernel, shape, scale, slot, others),
                    (low_term, low_tile, stat),
                    (block_order, owners),
                    (query_rows, ratio_rows, seen[slot], *(stats[one] for one in others)),
                    4,
                )
            else:
                terms[slot], soft[slot] = run(
                    functools.partial(term_kernel, slot, last),
                    (low_term, low_tile),
                    (),
                    (query_rows, ratio_rows, power[slot], grad[slot], norm),
                    2,
                )
            got[slot] = lax.ppermute(terms[slot], "seq", pairs(slot, True))
        own, query_out = run(
            functools.partial(own_kernel, 0.5 * scale, last),
            (term, rel),
            (),
            (
                *(query_rows, ratio_rows, power[0], grad[0], norm, both),
                *(one for slot in steps for one in (soft[slot], seen[slot])),
            ),
            2 + slots,
        )
        return own, list(got.values()), query_out

    def one_head(query_rows, ratio_rows, key_rows, value_rows):
        both = jnp.concatenate((key_rows, value_rows), axis=1)
        own, got, query_out = (many if slots > FEW else few)(query_rows, ratio_rows, both)
        key_out, value_out = run(
            functools.partial(sum_kernel, 0.5 * scale), (part, part), (), (both, own, *got), 0
        )
        return query_out.reshape(group, rows, head), key_out, value_out

    results = [
        one_head(
            query[g * group : (g + 1) * group].reshape(queries, head),
            ratio[g * group : (g + 1) * group].reshape(queries, head),
            keys[g],
            values[g],
        )
        for g in range(kv_heads)
    ]
    return (
        jnp.concatenate([one for one, _, _ in results], axis=0),
        jnp.stack([one for _, one, _ in results], axis=0),
        jnp.stack([one for _, _, one in results], axis=0),
    )


def solution(mesh):
    spec = P("head", ("groups", "seq"), None)
    return jax.shard_map(
        body,
        mesh=mesh,
        in_specs=(spec, spec, spec, spec, P("groups")),
        out_specs=(spec, spec, spec),
        check_vma=False,
    )
```

```python
import functools
import math

import jax
import jax.numpy as jnp
from jax import lax
from jax.experimental import pallas as pl
from jax.experimental.pallas import tpu as pltpu
from jax.sharding import PartitionSpec as P


F32 = jnp.float32
BF16 = jnp.bfloat16
HIDDEN = -1e30
FEW = 8
LOG2E = math.log2(math.e)
KEYS_FIRST = (2, 3, 1)
TERMS_FIRST = (3, 1, 2)


def dot(a, b, dims):
    return lax.dot_general(a, b, (dims, ((), ())), preferred_element_type=F32)


def folded(combine, tile):
    return combine(tile.reshape(tile.shape[0] // 8, 8, tile.shape[1]), axis=0)


def place_limits(shape, order_ref, mine, owner, queries):
    blocks, block_rows = shape
    lane = lax.broadcasted_iota(jnp.int32, (1, queries), 1) % (blocks * block_rows)
    places = lane % block_rows
    for block in range(blocks):
        first = order_ref[mine * blocks + block] * block_rows
        places = places + jnp.where(lane // block_rows == block, first, 0)
    return [places - order_ref[owner * blocks + block] * block_rows for block in range(blocks)]


def masked_scores(limits, query, keys):
    block_rows = keys.shape[0] // len(limits)
    inner = lax.broadcasted_iota(jnp.int32, (block_rows, query.shape[0]), 0)
    found = dot(keys, query, ((1,), (1,)))
    parts = []
    for block, limit in enumerate(limits):
        part = found[block * block_rows : (block + 1) * block_rows]
        parts.append(jnp.where(inner <= limit, part, HIDDEN))
    return jnp.concatenate(parts, axis=0)


def block_softmax(scale, limits, query, ratio, both):
    head = query.shape[1]
    found = masked_scores(limits, query, both[:, :head])
    top = jnp.max(folded(jnp.max, found), axis=0, keepdims=True)
    power = jnp.exp2((found - top) * (scale * LOG2E))
    grad = dot(both[:, head:], ratio, ((1,), (1,)))
    total = jnp.sum(folded(jnp.sum, power), axis=0, keepdims=True)
    weighted = jnp.sum(folded(jnp.sum, power * grad), axis=0, keepdims=True)
    return power, grad, (top, total, weighted)


def store_block(results, power_ref, grad_ref, stat_ref):
    power, grad, stats = results
    power_ref[...] = power
    grad_ref[...] = grad
    for row, stat in enumerate(stats):
        stat_ref[row : row + 1, :] = stat


def own_block_kernel(shape, scale, order_ref, owner_ref, query_ref, ratio_ref, both_ref, *rest):
    *outs, hide_ref = rest
    blocks, queries = shape[0], query_ref.shape[0]
    own = place_limits(shape, order_ref, owner_ref[0], owner_ref[0], queries)
    for slot in range(1, hide_ref.shape[0] // blocks):
        limits = place_limits(shape, order_ref, owner_ref[0], owner_ref[slot], queries)
        for block, limit in enumerate(limits):
            row = slot * blocks + block
            hide_ref[row : row + 1, :] = jnp.where(limit < 0, -HIDDEN, 0.0)
    results = block_softmax(scale, own, query_ref[...], ratio_ref[...], both_ref[...])
    store_block(results, *outs)


def finish(power, grad, share, expect, query, ratio):
    weights = power * share
    soft = (weights * (grad - expect)).astype(BF16)
    key_part = dot(soft, query, ((1,), (0,)))
    value_part = dot(weights.astype(BF16), ratio, ((1,), (0,)))
    return soft, key_part, value_part


def seen_softmax(scale, found, hides, top, grad):
    step = found.shape[0] // len(hides)
    parts = [found[row : row + step] for row in range(0, found.shape[0], step)]
    for part, hide in zip(parts, hides):
        own = jnp.max(folded(jnp.max, part), axis=0, keepdims=True) - hide
        top = jnp.maximum(top, own)
    power = jnp.concatenate(
        [jnp.exp2((part - (top + hide)) * (scale * LOG2E)) for part, hide in zip(parts, hides)],
        axis=0,
    )
    total = jnp.sum(folded(jnp.sum, power), axis=0, keepdims=True)
    weighted = jnp.sum(folded(jnp.sum, power * grad), axis=0, keepdims=True)
    return power, (top, total, weighted)


def block_kernel(blocks, scale, slot, hide_ref, query_ref, ratio_ref, both_ref, power_ref, grad_ref, stat_ref):
    hides = [hide_ref[row : row + 1, :] for row in range(slot * blocks, (slot + 1) * blocks)]
    head = query_ref.shape[1]
    found = dot(both_ref[:, :head], query_ref[...], ((1,), (1,)))
    grad = dot(both_ref[:, head:], ratio_ref[...], ((1,), (1,)))
    least = jnp.full((1, found.shape[1]), 0.1 * HIDDEN, F32)
    power, stats = seen_softmax(scale, found, hides, least, grad)
    store_block((power, grad, stats), power_ref, grad_ref, stat_ref)


def late_kernel(blocks, scale, order, late, width, hide_ref, query_ref, ratio_ref, *rest):
    early = [slot for slot in order if slot not in late]
    seen_refs, rest = rest[: len(late)], rest[len(late) :]
    stat_refs, rest = rest[: len(early) + 1], rest[len(early) + 1 :]
    tile_refs, rest = rest[: 2 * len(early)], rest[2 * len(early) :]
    term_ref, soft_ref, norm_ref, low_ref = rest
    rows = seen_refs[0].shape[0]
    queries, head = query_ref.shape
    keys = jnp.concatenate([ref[:, :head] for ref in seen_refs], axis=0)
    values = jnp.concatenate([ref[:, head:] for ref in seen_refs], axis=0)
    for start in range(0, queries, width):
        span = slice(start, start + width)
        hides = [
            hide_ref[row : row + 1, span]
            for slot in late
            for row in range(slot * blocks, (slot + 1) * blocks)
        ]
        stats = [[ref[row : row + 1, span] for row in range(3)] for ref in stat_refs]
        top = functools.reduce(jnp.maximum, [stat[0] for stat in stats])
        found = dot(keys, query_ref[span, :], ((1,), (1,)))
        grad = dot(values, ratio_ref[span, :], ((1,), (1,)))
        power, (top, total, weighted) = seen_softmax(scale, found, hides, top, grad)
        shares = [jnp.exp2((stat[0] - top) * (scale * LOG2E)) for stat in stats]
        for share, stat in zip(shares, stats):
            total = total + share * stat[1]
            weighted = weighted + share * stat[2]
        whole = 1.0 / total
        expect = weighted * whole
        norm_ref[0:1, span] = shares[0] * whole
        norm_ref[1:2, span] = expect
        for place, slot in enumerate(order):
            if slot in late:
                first = late.index(slot) * rows
                weights = power[first : first + rows] * whole
                slopes = grad[first : first + rows]
            else:
                one = early.index(slot)
                weights = tile_refs[2 * one][:, span] * (shares[one + 1] * whole)
                slopes = tile_refs[2 * one + 1][:, span]
            lines = slice(place * rows, (place + 1) * rows)
            soft_ref[lines, span] = (weights * (slopes - expect)).astype(BF16)
            low_ref[lines, span] = weights.astype(BF16)
    store_terms(soft_ref[:rows], low_ref[:rows], query_ref, ratio_ref, [term_ref])


def store_terms(soft, low, query_ref, ratio_ref, term_refs):
    head = query_ref.shape[1]
    key_part = dot(soft, query_ref[...], ((1,), (0,))).astype(BF16)
    value_part = dot(low, ratio_ref[...], ((1,), (0,))).astype(BF16)
    for place, term_ref in enumerate(term_refs):
        rows = term_ref.shape[0]
        term_ref[:, :head] = key_part[place * rows : (place + 1) * rows]
        term_ref[:, head:] = value_part[place * rows : (place + 1) * rows]


def rest_kernel(query_ref, ratio_ref, soft_ref, low_ref, *term_refs):
    rows = term_refs[0].shape[0]
    store_terms(soft_ref[rows:], low_ref[rows:], query_ref, ratio_ref, term_refs)


def own_kernel(factor, query_ref, ratio_ref, power_ref, grad_ref, norm_ref, both_ref, soft_ref, *rest):
    *seen_refs, own_ref, out_ref = rest
    head = query_ref.shape[1]
    soft, key_part, value_part = finish(
        power_ref[...],
        grad_ref[...],
        norm_ref[0:1, :],
        norm_ref[1:2, :],
        query_ref[...],
        ratio_ref[...],
    )
    own_ref[:, :head] = key_part
    own_ref[:, head:] = value_part
    keys = jnp.concatenate([ref[:, :head] for ref in seen_refs], axis=0)
    found = dot(soft, both_ref[:, :head], ((0,), (0,))) + dot(soft_ref[...], keys, ((0,), (0,)))
    out_ref[...] = factor * query_ref[...].astype(F32) * found


def sum_kernel(factor, both_ref, own_ref, *rest):
    *got, key_out, value_out = rest
    head = key_out.shape[1]
    total = own_ref[...]
    for one in got:
        total = total + one[...].astype(F32)
    key_out[...] = factor * both_ref[:, :head].astype(F32) * total[:, :head]
    value_out[...] = both_ref[:, head:].astype(F32) * total[:, head:]


def whole_kernel(shape, scale, order_ref, owner_ref, query_ref, ratio_ref, seen_ref, terms_ref, out_ref, score_ref, grad_ref):
    slots, blocks, block_rows = shape
    rows = blocks * block_rows
    queries, head = query_ref.shape
    query, ratio = query_ref[...], ratio_ref[...]

    def rows_of(slot):
        return pl.ds(pl.multiple_of(slot * rows, rows), rows)

    def scores(slot, top):
        limits = place_limits((blocks, block_rows), order_ref, owner_ref[0], slot, queries)
        found = masked_scores(limits, query, seen_ref[slot, :, :head])
        score_ref[rows_of(slot), :] = found
        grad_ref[rows_of(slot), :] = dot(seen_ref[slot, :, head:], ratio, ((1,), (1,)))
        return jnp.maximum(top, folded(jnp.max, found))

    top = lax.fori_loop(0, slots, scores, jnp.full((8, queries), HIDDEN, F32))
    top = jnp.max(top, axis=0, keepdims=True)
    zero = jnp.zeros((8, queries), F32)

    def exps(slot, sums):
        power = jnp.exp2((score_ref[rows_of(slot), :] - top) * (scale * LOG2E))
        score_ref[rows_of(slot), :] = power
        weighted = power * grad_ref[rows_of(slot), :]
        return sums[0] + folded(jnp.sum, power), sums[1] + folded(jnp.sum, weighted)

    total, weighted = lax.fori_loop(0, slots, exps, (zero, zero))
    share = 1.0 / jnp.sum(total, axis=0, keepdims=True)
    expect = jnp.sum(weighted, axis=0, keepdims=True) * share
    out_ref[...] = jnp.zeros_like(out_ref)

    def terms(slot, carry):
        soft, key_part, value_part = finish(
            score_ref[rows_of(slot), :], grad_ref[rows_of(slot), :], share, expect, query, ratio
        )
        terms_ref[slot, :, :head] = key_part
        terms_ref[slot, :, head:] = value_part
        out_ref[...] += dot(soft, seen_ref[slot, :, :head], ((0,), (0,)))
        return carry

    lax.fori_loop(0, slots, terms, 0)
    out_ref[...] = 0.5 * scale * query.astype(F32) * out_ref[...]


def body(query, keys, values, ratio, block_order):
    kv_heads, rows, head = keys.shape
    group = query.shape[0] // kv_heads
    queries = group * rows
    scale = head ** (-0.5)
    slots = lax.axis_size("seq")
    mine = lax.axis_index("seq")
    blocks = block_order.shape[0] // slots
    block_rows = rows // blocks
    shape = (blocks, block_rows)
    swap = slots & (slots - 1) == 0
    limit = min(60 << 20, (8 << 20) + 16 * slots * rows * queries)
    params = pltpu.CompilerParams(vmem_limit_bytes=limit)
    smem = pl.BlockSpec(memory_space=pltpu.SMEM)
    vmem = pl.BlockSpec(memory_space=pltpu.VMEM)
    tile = jax.ShapeDtypeStruct((rows, queries), F32)
    stat = jax.ShapeDtypeStruct((8, queries), F32)
    low_term = jax.ShapeDtypeStruct((rows, 2 * head), BF16)
    term = jax.ShapeDtypeStruct((rows, 2 * head), F32)
    part = jax.ShapeDtypeStruct((rows, head), F32)
    rel = jax.ShapeDtypeStruct((queries, head), F32)

    def run(kernel, outs, scalars, arrays, dots, scratch=()):
        single = not isinstance(outs, tuple)
        return pl.pallas_call(
            kernel,
            out_shape=outs,
            in_specs=[smem] * len(scalars) + [vmem] * len(arrays),
            out_specs=vmem if single else (vmem,) * len(outs),
            scratch_shapes=scratch,
            compiler_params=params,
            cost_estimate=pl.CostEstimate(
                flops=2 * dots * rows * queries * head,
                bytes_accessed=4 * dots * rows * queries,
                transcendentals=rows * queries,
            ),
        )(*scalars, *arrays)

    def pairs(step, back):
        if swap:
            return [(device, device ^ step) for device in range(slots)]
        step = -step if back else step
        return [(device, (device + step) % slots) for device in range(slots)]

    def many(query_rows, ratio_rows, both):
        seen = lax.all_gather(both, "seq")
        terms, query_out = run(
            functools.partial(whole_kernel, (slots, *shape), scale),
            (jax.ShapeDtypeStruct((slots, rows, 2 * head), F32), rel),
            (block_order, mine.reshape(1)),
            (query_rows, ratio_rows, seen),
            5 * slots,
            [pltpu.VMEM((slots * rows, queries), F32)] * 2,
        )
        own = lax.psum_scatter(terms, "seq", scatter_dimension=0, tiled=False)
        return own, [], query_out

    def few(query_rows, ratio_rows, both):
        steps = range(1, slots)
        first = KEYS_FIRST if slots == len(KEYS_FIRST) + 1 else tuple(steps)
        then = TERMS_FIRST if slots == len(TERMS_FIRST) + 1 else tuple(steps)
        seen = {0: both}
        for step in first:
            seen[step] = lax.ppermute(both, "seq", pairs(step, False))
        device = jnp.arange(slots, dtype=jnp.int32)
        owners = mine ^ device if swap else lax.rem(mine - device + slots, slots)
        power, grad, stats = {}, {}, {}
        power[0], grad[0], stats[0], hides = run(
            functools.partial(own_block_kernel, shape, scale),
            (tile, tile, stat, jax.ShapeDtypeStruct((slots * blocks, queries), F32)),
            (block_order, owners),
            (query_rows, ratio_rows, both),
            2,
        )
        width = math.gcd(queries, 256)
        got = []
        early = [slot for slot in then if slot == first[0]]
        late = [slot for slot in then if slot not in early]
        for slot in early:
            power[slot], grad[slot], stats[slot] = run(
                functools.partial(block_kernel, blocks, scale, slot),
                (tile, tile, stat),
                (),
                (hides, query_rows, ratio_rows, seen[slot]),
                2,
            )
        low_tiles = jax.ShapeDtypeStruct((len(then) * rows, queries), BF16)
        term_first, soft, norm, low = run(
            functools.partial(late_kernel, blocks, scale, then, late, width),
            (low_term, low_tiles, stat, low_tiles),
            (),
            (
                *(hides, query_rows, ratio_rows),
                *(seen[slot] for slot in late),
                *(stats[slot] for slot in (0, *early)),
                *(one for slot in early for one in (power[slot], grad[slot])),
            ),
            4 * len(then),
        )
        terms = [term_first]
        if then[1:]:
            terms += run(
                rest_kernel,
                (low_term,) * len(then[1:]),
                (),
                (query_rows, ratio_rows, soft, low),
                2 * len(then[1:]),
            )
        for slot, one in zip(then, terms):
            got.append(lax.ppermute(one, "seq", pairs(slot, True)))
        own, query_out = run(
            functools.partial(own_kernel, 0.5 * scale),
            (term, rel),
            (),
            (
                *(query_rows, ratio_rows, power[0], grad[0], norm, both, soft),
                *(seen[slot] for slot in then),
            ),
            2 + slots,
        )
        return own, got, query_out

    def one_head(query_rows, ratio_rows, key_rows, value_rows):
        both = jnp.concatenate((key_rows, value_rows), axis=1)
        own, got, query_out = (many if slots > FEW else few)(query_rows, ratio_rows, both)
        key_out, value_out = run(
            functools.partial(sum_kernel, 0.5 * scale), (part, part), (), (both, own, *got), 0
        )
        return query_out.reshape(group, rows, head), key_out, value_out

    results = [
        one_head(
            query[g * group : (g + 1) * group].reshape(queries, head),
            ratio[g * group : (g + 1) * group].reshape(queries, head),
            keys[g],
            values[g],
        )
        for g in range(kv_heads)
    ]
    return (
        jnp.concatenate([one for one, _, _ in results], axis=0),
        jnp.stack([one for _, one, _ in results], axis=0),
        jnp.stack([one for _, _, one in results], axis=0),
    )


def solution(mesh):
    spec = P("head", ("groups", "seq"), None)
    return jax.shard_map(
        body,
        mesh=mesh,
        in_specs=(spec, spec, spec, spec, P("groups")),
        out_specs=(spec, spec, spec),
        check_vma=False,
    )
```

```python
import functools
import math

import jax
import jax.numpy as jnp
from jax import lax
from jax.experimental import pallas as pl
from jax.experimental.pallas import tpu as pltpu
from jax.sharding import PartitionSpec as P


F32 = jnp.float32
BF16 = jnp.bfloat16
HIDDEN = -1e30
FEW = 8
LOG2E = math.log2(math.e)
KEYS_FIRST = (2, 3, 1)
TERMS_FIRST = (3, 1, 2)


def dot(a, b, dims):
    return lax.dot_general(a, b, (dims, ((), ())), preferred_element_type=F32)


def folded(combine, tile):
    return combine(tile.reshape(tile.shape[0] // 8, 8, tile.shape[1]), axis=0)


def place_limits(shape, order_ref, mine, owner, queries):
    blocks, block_rows = shape
    lane = lax.broadcasted_iota(jnp.int32, (1, queries), 1) % (blocks * block_rows)
    places = lane % block_rows
    for block in range(blocks):
        first = order_ref[mine * blocks + block] * block_rows
        places = places + jnp.where(lane // block_rows == block, first, 0)
    return [places - order_ref[owner * blocks + block] * block_rows for block in range(blocks)]


def masked_scores(limits, query, keys):
    block_rows = keys.shape[0] // len(limits)
    inner = lax.broadcasted_iota(jnp.int32, (block_rows, query.shape[0]), 0)
    found = dot(keys, query, ((1,), (1,)))
    parts = []
    for block, limit in enumerate(limits):
        part = found[block * block_rows : (block + 1) * block_rows]
        parts.append(jnp.where(inner <= limit, part, HIDDEN))
    return jnp.concatenate(parts, axis=0)


def block_softmax(scale, limits, query, ratio, both):
    head = query.shape[1]
    found = masked_scores(limits, query, both[:, :head])
    top = jnp.max(folded(jnp.max, found), axis=0, keepdims=True)
    power = jnp.exp2((found - top) * (scale * LOG2E))
    grad = dot(both[:, head:], ratio, ((1,), (1,)))
    total = jnp.sum(folded(jnp.sum, power), axis=0, keepdims=True)
    weighted = jnp.sum(folded(jnp.sum, power * grad), axis=0, keepdims=True)
    return power, grad, (top, total, weighted)


def store_block(results, power_ref, grad_ref, stat_ref):
    power, grad, stats = results
    power_ref[...] = power
    grad_ref[...] = grad
    for row, stat in enumerate(stats):
        stat_ref[row : row + 1, :] = stat


def own_block_kernel(shape, scale, order_ref, owner_ref, query_ref, ratio_ref, both_ref, *rest):
    *outs, hide_ref = rest
    blocks, queries = shape[0], query_ref.shape[0]
    own = place_limits(shape, order_ref, owner_ref[0], owner_ref[0], queries)
    for slot in range(1, hide_ref.shape[0] // blocks):
        limits = place_limits(shape, order_ref, owner_ref[0], owner_ref[slot], queries)
        for block, limit in enumerate(limits):
            row = slot * blocks + block
            hide_ref[row : row + 1, :] = jnp.where(limit < 0, -HIDDEN, 0.0)
    results = block_softmax(scale, own, query_ref[...], ratio_ref[...], both_ref[...])
    store_block(results, *outs)


def finish(power, grad, share, expect, query, ratio):
    weights = power * share
    soft = (weights * (grad - expect)).astype(BF16)
    key_part = dot(soft, query, ((1,), (0,)))
    value_part = dot(weights.astype(BF16), ratio, ((1,), (0,)))
    return soft, key_part, value_part


def seen_softmax(scale, found, hides, top, grad):
    step = found.shape[0] // len(hides)
    parts = [found[row : row + step] for row in range(0, found.shape[0], step)]
    for part, hide in zip(parts, hides):
        own = jnp.max(folded(jnp.max, part), axis=0, keepdims=True) - hide
        top = jnp.maximum(top, own)
    power = jnp.concatenate(
        [jnp.exp2((part - (top + hide)) * (scale * LOG2E)) for part, hide in zip(parts, hides)],
        axis=0,
    )
    total = jnp.sum(folded(jnp.sum, power), axis=0, keepdims=True)
    weighted = jnp.sum(folded(jnp.sum, power * grad), axis=0, keepdims=True)
    return power, (top, total, weighted)


def block_kernel(blocks, scale, slot, hide_ref, query_ref, ratio_ref, both_ref, power_ref, grad_ref, stat_ref):
    hides = [hide_ref[row : row + 1, :] for row in range(slot * blocks, (slot + 1) * blocks)]
    head = query_ref.shape[1]
    found = dot(both_ref[:, :head], query_ref[...], ((1,), (1,)))
    grad = dot(both_ref[:, head:], ratio_ref[...], ((1,), (1,)))
    least = jnp.full((1, found.shape[1]), 0.1 * HIDDEN, F32)
    power, stats = seen_softmax(scale, found, hides, least, grad)
    store_block((power, grad, stats), power_ref, grad_ref, stat_ref)


def late_kernel(blocks, scale, order, late, width, hide_ref, query_ref, ratio_ref, *rest):
    early = [slot for slot in order if slot not in late]
    seen_refs, rest = rest[: len(late)], rest[len(late) :]
    stat_refs, rest = rest[: len(early) + 1], rest[len(early) + 1 :]
    tile_refs, rest = rest[: 2 * len(early)], rest[2 * len(early) :]
    *term_refs, soft_ref, norm_ref, low_ref = rest
    rows = seen_refs[0].shape[0]
    queries, head = query_ref.shape
    keys = jnp.concatenate([ref[:, :head] for ref in seen_refs], axis=0)
    values = jnp.concatenate([ref[:, head:] for ref in seen_refs], axis=0)
    for start in range(0, queries, width):
        span = slice(start, start + width)
        hides = [
            hide_ref[row : row + 1, span]
            for slot in late
            for row in range(slot * blocks, (slot + 1) * blocks)
        ]
        stats = [[ref[row : row + 1, span] for row in range(3)] for ref in stat_refs]
        top = functools.reduce(jnp.maximum, [stat[0] for stat in stats])
        found = dot(keys, query_ref[span, :], ((1,), (1,)))
        grad = dot(values, ratio_ref[span, :], ((1,), (1,)))
        power, (top, total, weighted) = seen_softmax(scale, found, hides, top, grad)
        shares = [jnp.exp2((stat[0] - top) * (scale * LOG2E)) for stat in stats]
        for share, stat in zip(shares, stats):
            total = total + share * stat[1]
            weighted = weighted + share * stat[2]
        whole = 1.0 / total
        expect = weighted * whole
        norm_ref[0:1, span] = shares[0] * whole
        norm_ref[1:2, span] = expect
        for place, slot in enumerate(order):
            if slot in late:
                first = late.index(slot) * rows
                weights = power[first : first + rows] * whole
                slopes = grad[first : first + rows]
            else:
                one = early.index(slot)
                weights = tile_refs[2 * one][:, span] * (shares[one + 1] * whole)
                slopes = tile_refs[2 * one + 1][:, span]
            lines = slice(place * rows, (place + 1) * rows)
            soft_ref[lines, span] = (weights * (slopes - expect)).astype(BF16)
            low_ref[lines, span] = weights.astype(BF16)
    key_part = dot(soft_ref[...], query_ref[...], ((1,), (0,))).astype(BF16)
    value_part = dot(low_ref[...], ratio_ref[...], ((1,), (0,))).astype(BF16)
    for place, term_ref in enumerate(term_refs):
        term_ref[:, :head] = key_part[place * rows : (place + 1) * rows]
        term_ref[:, head:] = value_part[place * rows : (place + 1) * rows]


def own_kernel(factor, query_ref, ratio_ref, power_ref, grad_ref, norm_ref, both_ref, soft_ref, *rest):
    *seen_refs, own_ref, out_ref = rest
    head = query_ref.shape[1]
    soft, key_part, value_part = finish(
        power_ref[...],
        grad_ref[...],
        norm_ref[0:1, :],
        norm_ref[1:2, :],
        query_ref[...],
        ratio_ref[...],
    )
    own_ref[:, :head] = key_part
    own_ref[:, head:] = value_part
    keys = jnp.concatenate([ref[:, :head] for ref in seen_refs], axis=0)
    found = dot(soft, both_ref[:, :head], ((0,), (0,))) + dot(soft_ref[...], keys, ((0,), (0,)))
    out_ref[...] = factor * query_ref[...].astype(F32) * found


def presum_kernel(own_ref, *rest):
    *got, out_ref = rest
    total = own_ref[...]
    for one in got:
        total = total + one[...].astype(F32)
    out_ref[...] = total


def sum_kernel(factor, both_ref, own_ref, *rest):
    *got, key_out, value_out, key_ref, value_ref, sems = rest
    head = key_out.shape[1]
    copies = (
        pltpu.make_async_copy(key_ref, key_out, sems.at[0]),
        pltpu.make_async_copy(value_ref, value_out, sems.at[1]),
    )
    key_part = own_ref[:, :head]
    for one in got:
        key_part = key_part + one[:, :head].astype(F32)
    key_ref[...] = factor * both_ref[:, :head].astype(F32) * key_part
    copies[0].start()
    value_part = own_ref[:, head:]
    for one in got:
        value_part = value_part + one[:, head:].astype(F32)
    value_ref[...] = both_ref[:, head:].astype(F32) * value_part
    copies[1].start()
    copies[0].wait()
    copies[1].wait()


def whole_kernel(shape, scale, order_ref, owner_ref, query_ref, ratio_ref, seen_ref, terms_ref, out_ref, score_ref, grad_ref):
    slots, blocks, block_rows = shape
    rows = blocks * block_rows
    queries, head = query_ref.shape
    query, ratio = query_ref[...], ratio_ref[...]

    def rows_of(slot):
        return pl.ds(pl.multiple_of(slot * rows, rows), rows)

    def scores(slot, top):
        limits = place_limits((blocks, block_rows), order_ref, owner_ref[0], slot, queries)
        found = masked_scores(limits, query, seen_ref[slot, :, :head])
        score_ref[rows_of(slot), :] = found
        grad_ref[rows_of(slot), :] = dot(seen_ref[slot, :, head:], ratio, ((1,), (1,)))
        return jnp.maximum(top, folded(jnp.max, found))

    top = lax.fori_loop(0, slots, scores, jnp.full((8, queries), HIDDEN, F32))
    top = jnp.max(top, axis=0, keepdims=True)
    zero = jnp.zeros((8, queries), F32)

    def exps(slot, sums):
        power = jnp.exp2((score_ref[rows_of(slot), :] - top) * (scale * LOG2E))
        score_ref[rows_of(slot), :] = power
        weighted = power * grad_ref[rows_of(slot), :]
        return sums[0] + folded(jnp.sum, power), sums[1] + folded(jnp.sum, weighted)

    total, weighted = lax.fori_loop(0, slots, exps, (zero, zero))
    share = 1.0 / jnp.sum(total, axis=0, keepdims=True)
    expect = jnp.sum(weighted, axis=0, keepdims=True) * share
    out_ref[...] = jnp.zeros_like(out_ref)

    def terms(slot, carry):
        soft, key_part, value_part = finish(
            score_ref[rows_of(slot), :], grad_ref[rows_of(slot), :], share, expect, query, ratio
        )
        terms_ref[slot, :, :head] = key_part
        terms_ref[slot, :, head:] = value_part
        out_ref[...] += dot(soft, seen_ref[slot, :, :head], ((0,), (0,)))
        return carry

    lax.fori_loop(0, slots, terms, 0)
    out_ref[...] = 0.5 * scale * query.astype(F32) * out_ref[...]


def body(query, keys, values, ratio, block_order):
    kv_heads, rows, head = keys.shape
    group = query.shape[0] // kv_heads
    queries = group * rows
    scale = head ** (-0.5)
    slots = lax.axis_size("seq")
    mine = lax.axis_index("seq")
    blocks = block_order.shape[0] // slots
    block_rows = rows // blocks
    shape = (blocks, block_rows)
    swap = slots & (slots - 1) == 0
    limit = min(60 << 20, (8 << 20) + 16 * slots * rows * queries)
    params = pltpu.CompilerParams(vmem_limit_bytes=limit)
    smem = pl.BlockSpec(memory_space=pltpu.SMEM)
    vmem = pl.BlockSpec(memory_space=pltpu.VMEM)
    tile = jax.ShapeDtypeStruct((rows, queries), F32)
    stat = jax.ShapeDtypeStruct((8, queries), F32)
    low_term = jax.ShapeDtypeStruct((rows, 2 * head), BF16)
    term = jax.ShapeDtypeStruct((rows, 2 * head), F32)
    part = jax.ShapeDtypeStruct((rows, head), F32)
    rel = jax.ShapeDtypeStruct((queries, head), F32)

    def run(kernel, outs, scalars, arrays, dots, scratch=(), out_space=pltpu.VMEM):
        single = not isinstance(outs, tuple)
        space = pl.BlockSpec(memory_space=out_space)
        return pl.pallas_call(
            kernel,
            out_shape=outs,
            in_specs=[smem] * len(scalars) + [vmem] * len(arrays),
            out_specs=space if single else (space,) * len(outs),
            scratch_shapes=scratch,
            compiler_params=params,
            cost_estimate=pl.CostEstimate(
                flops=2 * dots * rows * queries * head,
                bytes_accessed=4 * dots * rows * queries,
                transcendentals=rows * queries,
            ),
        )(*scalars, *arrays)

    def pairs(step, back):
        if swap:
            return [(device, device ^ step) for device in range(slots)]
        step = -step if back else step
        return [(device, (device + step) % slots) for device in range(slots)]

    def many(query_rows, ratio_rows, both):
        seen = lax.all_gather(both, "seq")
        terms, query_out = run(
            functools.partial(whole_kernel, (slots, *shape), scale),
            (jax.ShapeDtypeStruct((slots, rows, 2 * head), F32), rel),
            (block_order, mine.reshape(1)),
            (query_rows, ratio_rows, seen),
            5 * slots,
            [pltpu.VMEM((slots * rows, queries), F32)] * 2,
        )
        own = lax.psum_scatter(terms, "seq", scatter_dimension=0, tiled=False)
        return own, [], query_out

    def few(query_rows, ratio_rows, both):
        steps = range(1, slots)
        first = KEYS_FIRST if slots == len(KEYS_FIRST) + 1 else tuple(steps)
        then = TERMS_FIRST if slots == len(TERMS_FIRST) + 1 else tuple(steps)
        seen = {0: both}
        for step in first:
            seen[step] = lax.ppermute(both, "seq", pairs(step, False))
        device = jnp.arange(slots, dtype=jnp.int32)
        owners = mine ^ device if swap else lax.rem(mine - device + slots, slots)
        power, grad, stats = {}, {}, {}
        power[0], grad[0], stats[0], hides = run(
            functools.partial(own_block_kernel, shape, scale),
            (tile, tile, stat, jax.ShapeDtypeStruct((slots * blocks, queries), F32)),
            (block_order, owners),
            (query_rows, ratio_rows, both),
            2,
        )
        width = math.gcd(queries, 256)
        got = []
        early = [slot for slot in then if slot == first[0]]
        late = [slot for slot in then if slot not in early]
        for slot in early:
            power[slot], grad[slot], stats[slot] = run(
                functools.partial(block_kernel, blocks, scale, slot),
                (tile, tile, stat),
                (),
                (hides, query_rows, ratio_rows, seen[slot]),
                2,
            )
        *terms, soft, norm = run(
            functools.partial(late_kernel, blocks, scale, then, late, width),
            (
                *[low_term] * len(then),
                jax.ShapeDtypeStruct((len(then) * rows, queries), BF16),
                stat,
            ),
            (),
            (
                *(hides, query_rows, ratio_rows),
                *(seen[slot] for slot in late),
                *(stats[slot] for slot in (0, *early)),
                *(one for slot in early for one in (power[slot], grad[slot])),
            ),
            4 * len(then),
            [pltpu.VMEM((len(then) * rows, queries), BF16)],
        )
        for slot, one in zip(then, terms):
            got.append(lax.ppermute(one, "seq", pairs(slot, True)))
        own, query_out = run(
            functools.partial(own_kernel, 0.5 * scale),
            (term, rel),
            (),
            (
                *(query_rows, ratio_rows, power[0], grad[0], norm, both, soft),
                *(seen[slot] for slot in then),
            ),
            2 + slots,
        )
        if got[1:]:
            own = run(presum_kernel, term, (), (own, *got[:-1]), 1)
        return own, got[-1:], query_out

    def one_head(query_rows, ratio_rows, key_rows, value_rows):
        both = jnp.concatenate((key_rows, value_rows), axis=1)
        own, got, query_out = (many if slots > FEW else few)(query_rows, ratio_rows, both)
        key_out, value_out = run(
            functools.partial(sum_kernel, 0.5 * scale),
            (part, part),
            (),
            (both, own, *got),
            0,
            [pltpu.VMEM((rows, head), F32)] * 2 + [pltpu.SemaphoreType.DMA((2,))],
            out_space=pltpu.HBM,
        )
        return query_out.reshape(group, rows, head), key_out, value_out

    results = [
        one_head(
            query[g * group : (g + 1) * group].reshape(queries, head),
            ratio[g * group : (g + 1) * group].reshape(queries, head),
            keys[g],
            values[g],
        )
        for g in range(kv_heads)
    ]
    return (
        jnp.concatenate([one for one, _, _ in results], axis=0),
        jnp.stack([one for _, one, _ in results], axis=0),
        jnp.stack([one for _, _, one in results], axis=0),
    )


def solution(mesh):
    spec = P("head", ("groups", "seq"), None)
    return jax.shard_map(
        body,
        mesh=mesh,
        in_specs=(spec, spec, spec, spec, P("groups")),
        out_specs=(spec, spec, spec),
        check_vma=False,
    )
```

```python
import functools
import math

import jax
import jax.numpy as jnp
from jax import lax
from jax.experimental import pallas as pl
from jax.experimental.pallas import tpu as pltpu
from jax.sharding import PartitionSpec as P


F32 = jnp.float32
BF16 = jnp.bfloat16
HIDDEN = -1e30
FEW = 8
LOG2E = math.log2(math.e)
KEYS_FIRST = (1, 2, 3)
TERMS_FIRST = (3, 2, 1)


def dot(a, b, dims):
    return lax.dot_general(a, b, (dims, ((), ())), preferred_element_type=F32)


def folded(combine, tile):
    return combine(tile.reshape(tile.shape[0] // 8, 8, tile.shape[1]), axis=0)


def place_limits(shape, order_ref, mine, owner, queries):
    blocks, block_rows = shape
    lane = lax.broadcasted_iota(jnp.int32, (1, queries), 1) % (blocks * block_rows)
    places = lane % block_rows
    for block in range(blocks):
        first = order_ref[mine * blocks + block] * block_rows
        places = places + jnp.where(lane // block_rows == block, first, 0)
    return [places - order_ref[owner * blocks + block] * block_rows for block in range(blocks)]


def masked_scores(limits, query, keys):
    block_rows = keys.shape[0] // len(limits)
    inner = lax.broadcasted_iota(jnp.int32, (block_rows, query.shape[0]), 0)
    found = dot(keys, query, ((1,), (1,)))
    parts = []
    for block, limit in enumerate(limits):
        part = found[block * block_rows : (block + 1) * block_rows]
        parts.append(jnp.where(inner <= limit, part, HIDDEN))
    return jnp.concatenate(parts, axis=0)


def block_softmax(scale, limits, query, ratio, both):
    head = query.shape[1]
    found = masked_scores(limits, query, both[:, :head])
    top = jnp.max(folded(jnp.max, found), axis=0, keepdims=True)
    power = jnp.exp2((found - top) * (scale * LOG2E))
    grad = dot(both[:, head:], ratio, ((1,), (1,)))
    total = jnp.sum(folded(jnp.sum, power), axis=0, keepdims=True)
    weighted = jnp.sum(folded(jnp.sum, power * grad), axis=0, keepdims=True)
    return power, grad, (top, total, weighted)


def store_block(results, power_ref, grad_ref, stat_ref):
    power, grad, stats = results
    power_ref[...] = power
    grad_ref[...] = grad
    for row, stat in enumerate(stats):
        stat_ref[row : row + 1, :] = stat


def own_block_kernel(shape, scale, order_ref, owner_ref, query_ref, ratio_ref, both_ref, *rest):
    *outs, hide_ref = rest
    blocks, queries = shape[0], query_ref.shape[0]
    own = place_limits(shape, order_ref, owner_ref[0], owner_ref[0], queries)
    for slot in range(1, hide_ref.shape[0] // blocks):
        limits = place_limits(shape, order_ref, owner_ref[0], owner_ref[slot], queries)
        for block, limit in enumerate(limits):
            row = slot * blocks + block
            hide_ref[row : row + 1, :] = jnp.where(limit < 0, -HIDDEN, 0.0)
    results = block_softmax(scale, own, query_ref[...], ratio_ref[...], both_ref[...])
    store_block(results, *outs)


def finish(power, grad, share, expect, query, ratio):
    weights = power * share
    soft = (weights * (grad - expect)).astype(BF16)
    key_part = dot(soft, query, ((1,), (0,)))
    value_part = dot(weights.astype(BF16), ratio, ((1,), (0,)))
    return soft, key_part, value_part


def seen_softmax(scale, found, hides, top, grad):
    step = found.shape[0] // len(hides)
    parts = [found[row : row + step] for row in range(0, found.shape[0], step)]
    for part, hide in zip(parts, hides):
        own = jnp.max(folded(jnp.max, part), axis=0, keepdims=True) - hide
        top = jnp.maximum(top, own)
    power = jnp.concatenate(
        [jnp.exp2((part - (top + hide)) * (scale * LOG2E)) for part, hide in zip(parts, hides)],
        axis=0,
    )
    total = jnp.sum(folded(jnp.sum, power), axis=0, keepdims=True)
    weighted = jnp.sum(folded(jnp.sum, power * grad), axis=0, keepdims=True)
    return power, (top, total, weighted)


def block_kernel(blocks, scale, slot, hide_ref, query_ref, ratio_ref, both_ref, power_ref, grad_ref, stat_ref):
    hides = [hide_ref[row : row + 1, :] for row in range(slot * blocks, (slot + 1) * blocks)]
    head = query_ref.shape[1]
    found = dot(both_ref[:, :head], query_ref[...], ((1,), (1,)))
    grad = dot(both_ref[:, head:], ratio_ref[...], ((1,), (1,)))
    least = jnp.full((1, found.shape[1]), 0.1 * HIDDEN, F32)
    power, stats = seen_softmax(scale, found, hides, least, grad)
    store_block((power, grad, stats), power_ref, grad_ref, stat_ref)


def late_kernel(blocks, scale, order, late, width, hide_ref, query_ref, ratio_ref, *rest):
    early = [slot for slot in order if slot not in late]
    seen_refs, rest = rest[: len(late)], rest[len(late) :]
    stat_refs, rest = rest[: len(early) + 1], rest[len(early) + 1 :]
    tile_refs, rest = rest[: 2 * len(early)], rest[2 * len(early) :]
    *term_refs, soft_ref, norm_ref, low_ref = rest
    rows = seen_refs[0].shape[0]
    queries, head = query_ref.shape
    keys = jnp.concatenate([ref[:, :head] for ref in seen_refs], axis=0)
    values = jnp.concatenate([ref[:, head:] for ref in seen_refs], axis=0)
    for start in range(0, queries, width):
        span = slice(start, start + width)
        hides = [
            hide_ref[row : row + 1, span]
            for slot in late
            for row in range(slot * blocks, (slot + 1) * blocks)
        ]
        stats = [[ref[row : row + 1, span] for row in range(3)] for ref in stat_refs]
        top = functools.reduce(jnp.maximum, [stat[0] for stat in stats])
        found = dot(keys, query_ref[span, :], ((1,), (1,)))
        grad = dot(values, ratio_ref[span, :], ((1,), (1,)))
        power, (top, total, weighted) = seen_softmax(scale, found, hides, top, grad)
        shares = [jnp.exp2((stat[0] - top) * (scale * LOG2E)) for stat in stats]
        for share, stat in zip(shares, stats):
            total = total + share * stat[1]
            weighted = weighted + share * stat[2]
        whole = 1.0 / total
        expect = weighted * whole
        norm_ref[0:1, span] = shares[0] * whole
        norm_ref[1:2, span] = expect
        for place, slot in enumerate(order):
            if slot in late:
                first = late.index(slot) * rows
                weights = power[first : first + rows] * whole
                slopes = grad[first : first + rows]
            else:
                one = early.index(slot)
                weights = tile_refs[2 * one][:, span] * (shares[one + 1] * whole)
                slopes = tile_refs[2 * one + 1][:, span]
            lines = slice(place * rows, (place + 1) * rows)
            soft_ref[lines, span] = (weights * (slopes - expect)).astype(BF16)
            low_ref[lines, span] = weights.astype(BF16)
    key_part = dot(soft_ref[...], query_ref[...], ((1,), (0,))).astype(BF16)
    value_part = dot(low_ref[...], ratio_ref[...], ((1,), (0,))).astype(BF16)
    for place, term_ref in enumerate(term_refs):
        term_ref[:, :head] = key_part[place * rows : (place + 1) * rows]
        term_ref[:, head:] = value_part[place * rows : (place + 1) * rows]


def own_kernel(factor, query_ref, ratio_ref, power_ref, grad_ref, norm_ref, both_ref, soft_ref, *rest):
    *seen_refs, own_ref, out_ref = rest
    head = query_ref.shape[1]
    soft, key_part, value_part = finish(
        power_ref[...],
        grad_ref[...],
        norm_ref[0:1, :],
        norm_ref[1:2, :],
        query_ref[...],
        ratio_ref[...],
    )
    own_ref[:, :head] = key_part
    own_ref[:, head:] = value_part
    keys = jnp.concatenate([ref[:, :head] for ref in seen_refs], axis=0)
    found = dot(soft, both_ref[:, :head], ((0,), (0,))) + dot(soft_ref[...], keys, ((0,), (0,)))
    out_ref[...] = factor * query_ref[...].astype(F32) * found


def sum_kernel(factor, both_ref, own_ref, *rest):
    *got, key_out, value_out = rest
    head = key_out.shape[1]
    total = own_ref[...]
    for one in got:
        total = total + one[...].astype(F32)
    key_out[...] = factor * both_ref[:, :head].astype(F32) * total[:, :head]
    value_out[...] = both_ref[:, head:].astype(F32) * total[:, head:]


def whole_kernel(shape, scale, order_ref, owner_ref, query_ref, ratio_ref, seen_ref, terms_ref, out_ref, score_ref, grad_ref):
    slots, blocks, block_rows = shape
    rows = blocks * block_rows
    queries, head = query_ref.shape
    query, ratio = query_ref[...], ratio_ref[...]

    def rows_of(slot):
        return pl.ds(pl.multiple_of(slot * rows, rows), rows)

    def scores(slot, top):
        limits = place_limits((blocks, block_rows), order_ref, owner_ref[0], slot, queries)
        found = masked_scores(limits, query, seen_ref[slot, :, :head])
        score_ref[rows_of(slot), :] = found
        grad_ref[rows_of(slot), :] = dot(seen_ref[slot, :, head:], ratio, ((1,), (1,)))
        return jnp.maximum(top, folded(jnp.max, found))

    top = lax.fori_loop(0, slots, scores, jnp.full((8, queries), HIDDEN, F32))
    top = jnp.max(top, axis=0, keepdims=True)
    zero = jnp.zeros((8, queries), F32)

    def exps(slot, sums):
        power = jnp.exp2((score_ref[rows_of(slot), :] - top) * (scale * LOG2E))
        score_ref[rows_of(slot), :] = power
        weighted = power * grad_ref[rows_of(slot), :]
        return sums[0] + folded(jnp.sum, power), sums[1] + folded(jnp.sum, weighted)

    total, weighted = lax.fori_loop(0, slots, exps, (zero, zero))
    share = 1.0 / jnp.sum(total, axis=0, keepdims=True)
    expect = jnp.sum(weighted, axis=0, keepdims=True) * share
    out_ref[...] = jnp.zeros_like(out_ref)

    def terms(slot, carry):
        soft, key_part, value_part = finish(
            score_ref[rows_of(slot), :], grad_ref[rows_of(slot), :], share, expect, query, ratio
        )
        terms_ref[slot, :, :head] = key_part
        terms_ref[slot, :, head:] = value_part
        out_ref[...] += dot(soft, seen_ref[slot, :, :head], ((0,), (0,)))
        return carry

    lax.fori_loop(0, slots, terms, 0)
    out_ref[...] = 0.5 * scale * query.astype(F32) * out_ref[...]


def body(query, keys, values, ratio, block_order):
    kv_heads, rows, head = keys.shape
    group = query.shape[0] // kv_heads
    queries = group * rows
    scale = head ** (-0.5)
    slots = lax.axis_size("seq")
    mine = lax.axis_index("seq")
    blocks = block_order.shape[0] // slots
    block_rows = rows // blocks
    shape = (blocks, block_rows)
    limit = min(60 << 20, (8 << 20) + 16 * slots * rows * queries)
    params = pltpu.CompilerParams(vmem_limit_bytes=limit)
    smem = pl.BlockSpec(memory_space=pltpu.SMEM)
    vmem = pl.BlockSpec(memory_space=pltpu.VMEM)
    tile = jax.ShapeDtypeStruct((rows, queries), F32)
    stat = jax.ShapeDtypeStruct((8, queries), F32)
    low_term = jax.ShapeDtypeStruct((rows, 2 * head), BF16)
    term = jax.ShapeDtypeStruct((rows, 2 * head), F32)
    part = jax.ShapeDtypeStruct((rows, head), F32)
    rel = jax.ShapeDtypeStruct((queries, head), F32)

    def run(kernel, outs, scalars, arrays, dots, scratch=()):
        single = not isinstance(outs, tuple)
        return pl.pallas_call(
            kernel,
            out_shape=outs,
            in_specs=[smem] * len(scalars) + [vmem] * len(arrays),
            out_specs=vmem if single else (vmem,) * len(outs),
            scratch_shapes=scratch,
            compiler_params=params,
            cost_estimate=pl.CostEstimate(
                flops=2 * dots * rows * queries * head,
                bytes_accessed=4 * dots * rows * queries,
                transcendentals=rows * queries,
            ),
        )(*scalars, *arrays)

    def pairs(step, back):
        step = -step if back else step
        return [(device, (device + step) % slots) for device in range(slots)]

    def many(query_rows, ratio_rows, both):
        seen = lax.all_gather(both, "seq")
        terms, query_out = run(
            functools.partial(whole_kernel, (slots, *shape), scale),
            (jax.ShapeDtypeStruct((slots, rows, 2 * head), F32), rel),
            (block_order, mine.reshape(1)),
            (query_rows, ratio_rows, seen),
            5 * slots,
            [pltpu.VMEM((slots * rows, queries), F32)] * 2,
        )
        own = lax.psum_scatter(terms, "seq", scatter_dimension=0, tiled=False)
        return own, [], query_out

    def few(query_rows, ratio_rows, both):
        steps = range(1, slots)
        first = KEYS_FIRST if slots == len(KEYS_FIRST) + 1 else tuple(steps)
        then = TERMS_FIRST if slots == len(TERMS_FIRST) + 1 else tuple(steps)
        seen = {0: both}
        for step in first:
            seen[step] = lax.ppermute(both, "seq", pairs(step, False))
        device = jnp.arange(slots, dtype=jnp.int32)
        owners = lax.rem(mine - device + slots, slots)
        power, grad, stats = {}, {}, {}
        power[0], grad[0], stats[0], hides = run(
            functools.partial(own_block_kernel, shape, scale),
            (tile, tile, stat, jax.ShapeDtypeStruct((slots * blocks, queries), F32)),
            (block_order, owners),
            (query_rows, ratio_rows, both),
            2,
        )
        width = math.gcd(queries, 256)
        got = []
        early = [slot for slot in then if slot == first[0]]
        late = [slot for slot in then if slot not in early]
        for slot in early:
            power[slot], grad[slot], stats[slot] = run(
                functools.partial(block_kernel, blocks, scale, slot),
                (tile, tile, stat),
                (),
                (hides, query_rows, ratio_rows, seen[slot]),
                2,
            )
        *terms, soft, norm = run(
            functools.partial(late_kernel, blocks, scale, then, late, width),
            (
                *[low_term] * len(then),
                jax.ShapeDtypeStruct((len(then) * rows, queries), BF16),
                stat,
            ),
            (),
            (
                *(hides, query_rows, ratio_rows),
                *(seen[slot] for slot in late),
                *(stats[slot] for slot in (0, *early)),
                *(one for slot in early for one in (power[slot], grad[slot])),
            ),
            4 * len(then),
            [pltpu.VMEM((len(then) * rows, queries), BF16)],
        )
        for slot, one in zip(then, terms):
            got.append(lax.ppermute(one, "seq", pairs(slot, True)))
        own, query_out = run(
            functools.partial(own_kernel, 0.5 * scale),
            (term, rel),
            (),
            (
                *(query_rows, ratio_rows, power[0], grad[0], norm, both, soft),
                *(seen[slot] for slot in then),
            ),
            2 + slots,
        )
        return own, got, query_out

    def one_head(query_rows, ratio_rows, key_rows, value_rows):
        both = jnp.concatenate((key_rows, value_rows), axis=1)
        own, got, query_out = (many if slots > FEW else few)(query_rows, ratio_rows, both)
        key_out, value_out = run(
            functools.partial(sum_kernel, 0.5 * scale), (part, part), (), (both, own, *got), 0
        )
        return query_out.reshape(group, rows, head), key_out, value_out

    results = [
        one_head(
            query[g * group : (g + 1) * group].reshape(queries, head),
            ratio[g * group : (g + 1) * group].reshape(queries, head),
            keys[g],
            values[g],
        )
        for g in range(kv_heads)
    ]
    return (
        jnp.concatenate([one for one, _, _ in results], axis=0),
        jnp.stack([one for _, one, _ in results], axis=0),
        jnp.stack([one for _, _, one in results], axis=0),
    )


def solution(mesh):
    spec = P("head", ("groups", "seq"), None)
    return jax.shard_map(
        body,
        mesh=mesh,
        in_specs=(spec, spec, spec, spec, P("groups")),
        out_specs=(spec, spec, spec),
        check_vma=False,
    )
```

```python
import functools
import math

import jax
import jax.numpy as jnp
from jax import lax
from jax.experimental import pallas as pl
from jax.experimental.pallas import tpu as pltpu
from jax.sharding import PartitionSpec as P


F32 = jnp.float32
BF16 = jnp.bfloat16
HIDDEN = -1e30
FEW = 8
LOG2E = math.log2(math.e)
KEYS_FIRST = (3, 1, 2)
TERMS_FIRST = (3, 2, 1)


def dot(a, b, dims):
    return lax.dot_general(a, b, (dims, ((), ())), preferred_element_type=F32)


def folded(combine, tile):
    return combine(tile.reshape(tile.shape[0] // 8, 8, tile.shape[1]), axis=0)


def place_limits(shape, order_ref, mine, owner, queries):
    blocks, block_rows = shape
    lane = lax.broadcasted_iota(jnp.int32, (1, queries), 1) % (blocks * block_rows)
    places = lane % block_rows
    for block in range(blocks):
        first = order_ref[mine * blocks + block] * block_rows
        places = places + jnp.where(lane // block_rows == block, first, 0)
    return [places - order_ref[owner * blocks + block] * block_rows for block in range(blocks)]


def masked_scores(limits, query, keys):
    block_rows = keys.shape[0] // len(limits)
    inner = lax.broadcasted_iota(jnp.int32, (block_rows, query.shape[0]), 0)
    found = dot(keys, query, ((1,), (1,)))
    parts = []
    for block, limit in enumerate(limits):
        part = found[block * block_rows : (block + 1) * block_rows]
        parts.append(jnp.where(inner <= limit, part, HIDDEN))
    return jnp.concatenate(parts, axis=0)


def block_softmax(scale, limits, query, ratio, both):
    head = query.shape[1]
    found = masked_scores(limits, query, both[:, :head])
    top = jnp.max(folded(jnp.max, found), axis=0, keepdims=True)
    power = jnp.exp2((found - top) * (scale * LOG2E))
    grad = dot(both[:, head:], ratio, ((1,), (1,)))
    total = jnp.sum(folded(jnp.sum, power), axis=0, keepdims=True)
    weighted = jnp.sum(folded(jnp.sum, power * grad), axis=0, keepdims=True)
    return power, grad, (top, total, weighted)


def store_block(results, power_ref, grad_ref, stat_ref):
    power, grad, stats = results
    power_ref[...] = power
    grad_ref[...] = grad
    for row, stat in enumerate(stats):
        stat_ref[row : row + 1, :] = stat


def own_block_kernel(shape, scale, order_ref, owner_ref, query_ref, ratio_ref, both_ref, *rest):
    *outs, hide_ref = rest
    blocks, queries = shape[0], query_ref.shape[0]
    own = place_limits(shape, order_ref, owner_ref[0], owner_ref[0], queries)
    for slot in range(1, hide_ref.shape[0] // blocks):
        limits = place_limits(shape, order_ref, owner_ref[0], owner_ref[slot], queries)
        for block, limit in enumerate(limits):
            row = slot * blocks + block
            hide_ref[row : row + 1, :] = jnp.where(limit < 0, -HIDDEN, 0.0)
    results = block_softmax(scale, own, query_ref[...], ratio_ref[...], both_ref[...])
    store_block(results, *outs)


def finish(power, grad, share, expect, query, ratio):
    weights = power * share
    soft = (weights * (grad - expect)).astype(BF16)
    key_part = dot(soft, query, ((1,), (0,)))
    value_part = dot(weights.astype(BF16), ratio, ((1,), (0,)))
    return soft, key_part, value_part


def seen_softmax(scale, found, hides, top, grad):
    step = found.shape[0] // len(hides)
    parts = [found[row : row + step] for row in range(0, found.shape[0], step)]
    for part, hide in zip(parts, hides):
        own = jnp.max(folded(jnp.max, part), axis=0, keepdims=True) - hide
        top = jnp.maximum(top, own)
    power = jnp.concatenate(
        [jnp.exp2((part - (top + hide)) * (scale * LOG2E)) for part, hide in zip(parts, hides)],
        axis=0,
    )
    total = jnp.sum(folded(jnp.sum, power), axis=0, keepdims=True)
    weighted = jnp.sum(folded(jnp.sum, power * grad), axis=0, keepdims=True)
    return power, (top, total, weighted)


def block_kernel(blocks, scale, slot, hide_ref, query_ref, ratio_ref, both_ref, power_ref, grad_ref, stat_ref):
    hides = [hide_ref[row : row + 1, :] for row in range(slot * blocks, (slot + 1) * blocks)]
    head = query_ref.shape[1]
    found = dot(both_ref[:, :head], query_ref[...], ((1,), (1,)))
    grad = dot(both_ref[:, head:], ratio_ref[...], ((1,), (1,)))
    least = jnp.full((1, found.shape[1]), 0.1 * HIDDEN, F32)
    power, stats = seen_softmax(scale, found, hides, least, grad)
    store_block((power, grad, stats), power_ref, grad_ref, stat_ref)


def late_kernel(blocks, scale, order, late, width, hide_ref, query_ref, ratio_ref, *rest):
    early = [slot for slot in order if slot not in late]
    seen_refs, rest = rest[: len(late)], rest[len(late) :]
    stat_refs, rest = rest[: len(early) + 1], rest[len(early) + 1 :]
    tile_refs, rest = rest[: 2 * len(early)], rest[2 * len(early) :]
    *term_refs, soft_ref, norm_ref, low_ref = rest
    rows = seen_refs[0].shape[0]
    queries, head = query_ref.shape
    keys = jnp.concatenate([ref[:, :head] for ref in seen_refs], axis=0)
    values = jnp.concatenate([ref[:, head:] for ref in seen_refs], axis=0)
    for start in range(0, queries, width):
        span = slice(start, start + width)
        hides = [
            hide_ref[row : row + 1, span]
            for slot in late
            for row in range(slot * blocks, (slot + 1) * blocks)
        ]
        stats = [[ref[row : row + 1, span] for row in range(3)] for ref in stat_refs]
        top = functools.reduce(jnp.maximum, [stat[0] for stat in stats])
        found = dot(keys, query_ref[span, :], ((1,), (1,)))
        grad = dot(values, ratio_ref[span, :], ((1,), (1,)))
        power, (top, total, weighted) = seen_softmax(scale, found, hides, top, grad)
        shares = [jnp.exp2((stat[0] - top) * (scale * LOG2E)) for stat in stats]
        for share, stat in zip(shares, stats):
            total = total + share * stat[1]
            weighted = weighted + share * stat[2]
        whole = 1.0 / total
        expect = weighted * whole
        norm_ref[0:1, span] = shares[0] * whole
        norm_ref[1:2, span] = expect
        for place, slot in enumerate(order):
            if slot in late:
                first = late.index(slot) * rows
                weights = power[first : first + rows] * whole
                slopes = grad[first : first + rows]
            else:
                one = early.index(slot)
                weights = tile_refs[2 * one][:, span] * (shares[one + 1] * whole)
                slopes = tile_refs[2 * one + 1][:, span]
            lines = slice(place * rows, (place + 1) * rows)
            soft_ref[lines, span] = (weights * (slopes - expect)).astype(BF16)
            low_ref[lines, span] = weights.astype(BF16)
    key_part = dot(soft_ref[...], query_ref[...], ((1,), (0,))).astype(BF16)
    value_part = dot(low_ref[...], ratio_ref[...], ((1,), (0,))).astype(BF16)
    for place, term_ref in enumerate(term_refs):
        term_ref[:, :head] = key_part[place * rows : (place + 1) * rows]
        term_ref[:, head:] = value_part[place * rows : (place + 1) * rows]


def own_kernel(factor, query_ref, ratio_ref, power_ref, grad_ref, norm_ref, both_ref, soft_ref, *rest):
    *seen_refs, own_ref, out_ref = rest
    head = query_ref.shape[1]
    soft, key_part, value_part = finish(
        power_ref[...],
        grad_ref[...],
        norm_ref[0:1, :],
        norm_ref[1:2, :],
        query_ref[...],
        ratio_ref[...],
    )
    own_ref[:, :head] = key_part
    own_ref[:, head:] = value_part
    keys = jnp.concatenate([ref[:, :head] for ref in seen_refs], axis=0)
    found = dot(soft, both_ref[:, :head], ((0,), (0,))) + dot(soft_ref[...], keys, ((0,), (0,)))
    out_ref[...] = factor * query_ref[...].astype(F32) * found


def sum_kernel(factor, both_ref, own_ref, *rest):
    *got, key_out, value_out = rest
    head = key_out.shape[1]
    total = own_ref[...]
    for one in got:
        total = total + one[...].astype(F32)
    key_out[...] = factor * both_ref[:, :head].astype(F32) * total[:, :head]
    value_out[...] = both_ref[:, head:].astype(F32) * total[:, head:]


def whole_kernel(shape, scale, order_ref, owner_ref, query_ref, ratio_ref, seen_ref, terms_ref, out_ref, score_ref, grad_ref):
    slots, blocks, block_rows = shape
    rows = blocks * block_rows
    queries, head = query_ref.shape
    query, ratio = query_ref[...], ratio_ref[...]

    def rows_of(slot):
        return pl.ds(pl.multiple_of(slot * rows, rows), rows)

    def scores(slot, top):
        limits = place_limits((blocks, block_rows), order_ref, owner_ref[0], slot, queries)
        found = masked_scores(limits, query, seen_ref[slot, :, :head])
        score_ref[rows_of(slot), :] = found
        grad_ref[rows_of(slot), :] = dot(seen_ref[slot, :, head:], ratio, ((1,), (1,)))
        return jnp.maximum(top, folded(jnp.max, found))

    top = lax.fori_loop(0, slots, scores, jnp.full((8, queries), HIDDEN, F32))
    top = jnp.max(top, axis=0, keepdims=True)
    zero = jnp.zeros((8, queries), F32)

    def exps(slot, sums):
        power = jnp.exp2((score_ref[rows_of(slot), :] - top) * (scale * LOG2E))
        score_ref[rows_of(slot), :] = power
        weighted = power * grad_ref[rows_of(slot), :]
        return sums[0] + folded(jnp.sum, power), sums[1] + folded(jnp.sum, weighted)

    total, weighted = lax.fori_loop(0, slots, exps, (zero, zero))
    share = 1.0 / jnp.sum(total, axis=0, keepdims=True)
    expect = jnp.sum(weighted, axis=0, keepdims=True) * share
    out_ref[...] = jnp.zeros_like(out_ref)

    def terms(slot, carry):
        soft, key_part, value_part = finish(
            score_ref[rows_of(slot), :], grad_ref[rows_of(slot), :], share, expect, query, ratio
        )
        terms_ref[slot, :, :head] = key_part
        terms_ref[slot, :, head:] = value_part
        out_ref[...] += dot(soft, seen_ref[slot, :, :head], ((0,), (0,)))
        return carry

    lax.fori_loop(0, slots, terms, 0)
    out_ref[...] = 0.5 * scale * query.astype(F32) * out_ref[...]


def body(query, keys, values, ratio, block_order):
    kv_heads, rows, head = keys.shape
    group = query.shape[0] // kv_heads
    queries = group * rows
    scale = head ** (-0.5)
    slots = lax.axis_size("seq")
    mine = lax.axis_index("seq")
    blocks = block_order.shape[0] // slots
    block_rows = rows // blocks
    shape = (blocks, block_rows)
    swap = slots & (slots - 1) == 0
    limit = min(60 << 20, (8 << 20) + 16 * slots * rows * queries)
    params = pltpu.CompilerParams(vmem_limit_bytes=limit)
    smem = pl.BlockSpec(memory_space=pltpu.SMEM)
    vmem = pl.BlockSpec(memory_space=pltpu.VMEM)
    tile = jax.ShapeDtypeStruct((rows, queries), F32)
    stat = jax.ShapeDtypeStruct((8, queries), F32)
    low_term = jax.ShapeDtypeStruct((rows, 2 * head), BF16)
    term = jax.ShapeDtypeStruct((rows, 2 * head), F32)
    part = jax.ShapeDtypeStruct((rows, head), F32)
    rel = jax.ShapeDtypeStruct((queries, head), F32)

    def run(kernel, outs, scalars, arrays, dots, scratch=()):
        single = not isinstance(outs, tuple)
        return pl.pallas_call(
            kernel,
            out_shape=outs,
            in_specs=[smem] * len(scalars) + [vmem] * len(arrays),
            out_specs=vmem if single else (vmem,) * len(outs),
            scratch_shapes=scratch,
            compiler_params=params,
            cost_estimate=pl.CostEstimate(
                flops=2 * dots * rows * queries * head,
                bytes_accessed=4 * dots * rows * queries,
                transcendentals=rows * queries,
            ),
        )(*scalars, *arrays)

    def pairs(step, back):
        if swap:
            return [(device, device ^ step) for device in range(slots)]
        step = -step if back else step
        return [(device, (device + step) % slots) for device in range(slots)]

    def many(query_rows, ratio_rows, both):
        seen = lax.all_gather(both, "seq")
        terms, query_out = run(
            functools.partial(whole_kernel, (slots, *shape), scale),
            (jax.ShapeDtypeStruct((slots, rows, 2 * head), F32), rel),
            (block_order, mine.reshape(1)),
            (query_rows, ratio_rows, seen),
            5 * slots,
            [pltpu.VMEM((slots * rows, queries), F32)] * 2,
        )
        own = lax.psum_scatter(terms, "seq", scatter_dimension=0, tiled=False)
        return own, [], query_out

    def few(query_rows, ratio_rows, both):
        steps = range(1, slots)
        first = KEYS_FIRST if slots == len(KEYS_FIRST) + 1 else tuple(steps)
        then = TERMS_FIRST if slots == len(TERMS_FIRST) + 1 else tuple(steps)
        seen = {0: both}
        for step in first:
            seen[step] = lax.ppermute(both, "seq", pairs(step, False))
        device = jnp.arange(slots, dtype=jnp.int32)
        owners = mine ^ device if swap else lax.rem(mine - device + slots, slots)
        power, grad, stats = {}, {}, {}
        power[0], grad[0], stats[0], hides = run(
            functools.partial(own_block_kernel, shape, scale),
            (tile, tile, stat, jax.ShapeDtypeStruct((slots * blocks, queries), F32)),
            (block_order, owners),
            (query_rows, ratio_rows, both),
            2,
        )
        width = math.gcd(queries, 256)
        got = []
        early = [slot for slot in then if slot == first[0]]
        late = [slot for slot in then if slot not in early]
        for slot in early:
            power[slot], grad[slot], stats[slot] = run(
                functools.partial(block_kernel, blocks, scale, slot),
                (tile, tile, stat),
                (),
                (hides, query_rows, ratio_rows, seen[slot]),
                2,
            )
        *terms, soft, norm = run(
            functools.partial(late_kernel, blocks, scale, then, late, width),
            (
                *[low_term] * len(then),
                jax.ShapeDtypeStruct((len(then) * rows, queries), BF16),
                stat,
            ),
            (),
            (
                *(hides, query_rows, ratio_rows),
                *(seen[slot] for slot in late),
                *(stats[slot] for slot in (0, *early)),
                *(one for slot in early for one in (power[slot], grad[slot])),
            ),
            4 * len(then),
            [pltpu.VMEM((len(then) * rows, queries), BF16)],
        )
        for slot, one in zip(then, terms):
            got.append(lax.ppermute(one, "seq", pairs(slot, True)))
        own, query_out = run(
            functools.partial(own_kernel, 0.5 * scale),
            (term, rel),
            (),
            (
                *(query_rows, ratio_rows, power[0], grad[0], norm, both, soft),
                *(seen[slot] for slot in then),
            ),
            2 + slots,
        )
        return own, got, query_out

    def one_head(query_rows, ratio_rows, key_rows, value_rows):
        both = jnp.concatenate((key_rows, value_rows), axis=1)
        own, got, query_out = (many if slots > FEW else few)(query_rows, ratio_rows, both)
        key_out, value_out = run(
            functools.partial(sum_kernel, 0.5 * scale), (part, part), (), (both, own, *got), 0
        )
        return query_out.reshape(group, rows, head), key_out, value_out

    results = [
        one_head(
            query[g * group : (g + 1) * group].reshape(queries, head),
            ratio[g * group : (g + 1) * group].reshape(queries, head),
            keys[g],
            values[g],
        )
        for g in range(kv_heads)
    ]
    return (
        jnp.concatenate([one for one, _, _ in results], axis=0),
        jnp.stack([one for _, one, _ in results], axis=0),
        jnp.stack([one for _, _, one in results], axis=0),
    )


def solution(mesh):
    spec = P("head", ("groups", "seq"), None)
    return jax.shard_map(
        body,
        mesh=mesh,
        in_specs=(spec, spec, spec, spec, P("groups")),
        out_specs=(spec, spec, spec),
        check_vma=False,
    )
```
